32 devices in a mesh: ctx: 8 (over z, x), kv: 4 (over y, core).
Axes of the slice: x: 2, y: 2, z: 4, core: 2. Of those that a mesh axis runs over, the one named last changes fastest.
Arguments:
- tokens: bfloat16 [4096, 2048], P(('ctx', 'kv')), may hold values from -6 to 6
- w_router: bfloat16 [2048, 32], replicated, may hold values from -0.0625 to 0.0625
- expert_ids: int32 [4096, 8], P(('ctx', 'kv')), may hold values from 0 to 31, all different within a row; in each aligned block of 128 rows (0 to 127, 128 to 255, ...) at most 40 rows name the same one
- w_gate: bfloat16 [32, 2048, 768], P(('ctx', 'kv')), may hold values from -0.125 to 0.125
- w_up: bfloat16 [32, 2048, 768], P(('ctx', 'kv')), may hold values from -0.125 to 0.125
- w_down: bfloat16 [32, 768, 2048], P(('ctx', 'kv')), may hold values from -0.21875 to 0.21875
- moe_gain: float32 [2048], replicated, may hold values from 0.1 to 1.9
- attn_gain: float32 [2048], replicated, may hold values from 0.1 to 1.9
- w_query: bfloat16 [2048, 4096], P(None, 'kv'), may hold values from -0.088388348 to 0.088388348
- w_key: bfloat16 [2048, 512], P(None, 'kv'), may hold values from -0.10606602 to 0.10606602
- w_value: bfloat16 [2048, 512], P(None, 'kv'), may hold values from -0.125 to 0.125
- w_out: bfloat16 [4096, 2048], P('kv'), may hold values from -0.5 to 0.5
- q_gain: float32 [128], replicated, may hold values from 1 to 6
- k_gain: float32 [128], replicated, may hold values from 1 to 6
Outputs:
- moe_out: bfloat16 [4096, 2048], P(('ctx', 'kv'))
- attended: bfloat16 [4096, 2048], P(('ctx', 'kv'))
The draws below stay inside these ranges and needn't reach their ends.
Inputs may be any that keep to these rules, and one draw needn't show every extreme that they name: `expert_ids`: each row names 8 different experts; in the 128 rows of one device no expert is named more than 40 times, and in every draw some expert is named exactly 40 times in the rows of some device.
All inputs are finite; a program needn't handle non-finite values.
Results may differ from the reference program's by a relative error of at most 0.03.
The reference program's roundings to bfloat16 on the way count: a program that leaves them out, or rounds other values in their place, can miss the bound.
Values may be sent and summed in bfloat16 or wider, within the bound.
No kernel may reach another device: no remote copies, remote signals or barrier semaphores. Data moves between devices by JAX's collectives and lax.ppermute only.
A program may use at most 192 MiB of HBM per device.

```python
import math
import jax
import jax.numpy as jnp
import numpy as np
from jax import lax

D = 2048
FF = 768
HEADS = 32
KV_HEADS = 4
HEAD_DIM = 128
TOP = 8
SEQ_DEV = 512
STOPS = 8
EXPERTS = 32
ROWS = 128
TOKENS = 4096
CAP = 40
N_CTX = 8
N_KV = 4


def paired_projections(key):
    query_weight = jax.random.truncated_normal(jax.random.fold_in(key, 11), -4.0, 4.0, (D, HEADS * HEAD_DIM), jnp.float32) / jnp.sqrt(jnp.float32(D))
    key_weight = jax.random.truncated_normal(jax.random.fold_in(key, 12), -4.0, 4.0, (D, KV_HEADS * HEAD_DIM), jnp.float32) / jnp.sqrt(jnp.float32(D))
    return (query_weight, key_weight)


def draw_w_query(key, part):
    return paired_projections(key)[0].astype(jnp.bfloat16)


def draw_w_key(key, part):
    return paired_projections(key)[1].astype(jnp.bfloat16)


def norm_gain(key, salt):
    values = jax.random.uniform(jax.random.fold_in(key, salt), (HEAD_DIM,), jnp.float32, 1.0, 2.0)
    return values


def draw_q_gain(key, part):
    return norm_gain(key, 21)


def draw_k_gain(key, part):
    return norm_gain(key, 22)


def levels(rng, dims, pieces, least, high):
    def one(position, parts):
        heights = jax.random.uniform(jax.random.fold_in(jax.random.fold_in(rng, 6), position), (parts,), jnp.float32, least / len(pieces), high / len(pieces))
        return jnp.repeat(jnp.exp(heights), dims[position] // parts).reshape((-1,) + (1,) * (len(dims) - position - 1))

    loudness = one(*pieces[0])
    for cut in pieces[1:]:
        loudness = loudness * one(*cut)
    return loudness


def assign_block(key, own, number, rows, count, top, limit, lean):
    ranking = jax.random.permutation(key, count)
    packed, common = portions_of(count, rows * top, limit, lean, True), portions_of(count, rows * top, limit, lean, False)
    places = jnp.arange(count)

    def named(lengths, rotation):
        used = int((lengths > 0).sum())
        fixed = max(1, used // 4)
        shifted = fixed + (places - fixed + rotation * (used - fixed)) % max(1, count - fixed)
        return jnp.zeros((count,), jnp.int32).at[ranking[jnp.where(places < fixed, places, shifted)]].set(jnp.asarray(lengths, jnp.int32))

    lengths = jnp.where(number % 4 == 0, named(packed, number // 4), named(common, number - number // 4 - 1))
    mixed = jax.random.permutation(jax.random.fold_in(own, 3), count)
    donor, sink = mixed[0:count // 2 * 2:2], mixed[1:count // 2 * 2:2]
    room = jnp.minimum(lengths[donor] - 1, limit - lengths[sink]) // 2
    room = jnp.where((donor == ranking[0]) | (sink == ranking[0]) | (lengths[sink] == 0), 0, jnp.maximum(room, 0))
    shifted = jax.random.randint(jax.random.fold_in(own, 4), (count // 2,), 0, 1 << 20) % (room + 1)
    lengths = lengths.at[donor].add(-shifted).at[sink].add(shifted)
    members = jnp.searchsorted(jnp.cumsum(lengths), jnp.arange(rows * top), side="right").astype(jnp.int32)
    listing = members.reshape(top, rows).T
    listing = listing[jax.random.permutation(jax.random.fold_in(own, 1), rows)]
    rotation = jax.random.randint(jax.random.fold_in(own, 2), (rows, 1), 0, top)
    return jnp.take_along_axis(listing, (jnp.arange(top)[None, :] + rotation) % top, axis=1)


def portions_of(amount, total, limit, lean, full):
    weights = [(1 << 20) // math.isqrt(standing ** lean) + 1 for standing in range(1, amount + 1)]
    largest = limit if full else min(limit, max(-(-total // amount), total * weights[0] // sum(weights)))
    least = 1 if total - largest >= amount - 1 else 0
    counts, rest = [largest] + [least] * (amount - 1), total - largest - least * (amount - 1)
    while rest > 0:
        candidates = [i for i in range(1, amount) if counts[i] < largest] or [i for i in range(1, amount) if counts[i] < limit]
        pool, budget = sum([weights[i] for i in candidates]), rest
        for i in candidates:
            addition = min(limit - counts[i], max(1, budget * weights[i] // pool), rest)
            counts[i] = counts[i] + addition
            rest = rest - addition
    return np.array(counts)


def bell_draw(key, extent, deviation, reach, cuts=(), kind=jnp.bfloat16):
    loudness = levels(key, extent, cuts, -0.22, 0.18) if cuts else 1.0
    values = jax.random.normal(key, extent, jnp.float32) * deviation * loudness
    return jnp.minimum(jnp.maximum(values, -reach), reach).astype(kind)


def setup_inputs(seed: int = 0) -> dict:
    streams_of = jax.random.split(jax.random.key(seed), 15)
    tokens = bell_draw(streams_of[0], (TOKENS, D), 1.0, 6.0, ((0, 32),))
    w_router = bell_draw(streams_of[1], (D, EXPERTS), (4 * D) ** -0.5, 0.0625)
    expert_ids_keys = jax.random.split(jax.random.fold_in(streams_of[2], 1), TOKENS // ROWS)
    expert_ids_turns = jax.random.permutation(jax.random.fold_in(streams_of[2], 3), TOKENS // ROWS)
    expert_ids = jax.vmap(lambda own, number: assign_block(jax.random.fold_in(streams_of[2], 2), own, number, ROWS, EXPERTS, TOP, CAP, 1))(expert_ids_keys, expert_ids_turns).reshape((TOKENS, TOP))
    w_gate = bell_draw(streams_of[3], (EXPERTS, D, FF), D ** -0.5, 0.125, ((0, 32),))
    w_up = bell_draw(streams_of[4], (EXPERTS, D, FF), D ** -0.5, 0.125, ((0, 32),))
    w_down = bell_draw(streams_of[5], (EXPERTS, FF, D), FF ** -0.5, 0.21875, ((0, 32),))
    moe_gain = jnp.clip(1.0 + 0.18 * jax.random.normal(streams_of[6], (D,), jnp.float32), 0.1, 1.9)
    attn_gain = jnp.clip(1.0 + 0.18 * jax.random.normal(streams_of[7], (D,), jnp.float32), 0.1, 1.9)
    w_query = draw_w_query(jax.random.fold_in(streams_of[14], 71), 0)
    w_key = draw_w_key(jax.random.fold_in(streams_of[14], 71), 0)
    w_value = bell_draw(streams_of[10], (D, KV_HEADS * HEAD_DIM), D ** -0.5, 0.125, ((1, 4),))
    w_out = bell_draw(streams_of[11], (HEADS * HEAD_DIM, D), HEAD_DIM ** -0.5, 0.5, ((0, 4),))
    q_gain = draw_q_gain(jax.random.fold_in(streams_of[14], 71), 0)
    k_gain = draw_k_gain(jax.random.fold_in(streams_of[14], 71), 0)
    return {"tokens": tokens, "w_router": w_router, "expert_ids": expert_ids, "w_gate": w_gate, "w_up": w_up, "w_down": w_down, "moe_gain": moe_gain, "attn_gain": attn_gain, "w_query": w_query, "w_key": w_key, "w_value": w_value, "w_out": w_out, "q_gain": q_gain, "k_gain": k_gain}


EPSILON = 1e-06
THETA = 1000000.0
MASKED = -1e+30

def rms_norm(values, scaling):
    values = values.astype(jnp.float32)
    inverse = lax.rsqrt(lax.optimization_barrier(jnp.mean(values * values, axis=-1, keepdims=True)) + EPSILON)
    return values * inverse * scaling.astype(jnp.float32)

def rotate(values, positions):
    half_width = values.shape[-1] // 2
    frequency = THETA ** (-2.0 * jnp.arange(half_width, dtype=jnp.float32) / values.shape[-1])
    angles = positions.astype(jnp.float32)[:, None] * frequency[None, :]
    cosine_table = jnp.cos(angles)[:, None, :]
    sine_table = jnp.sin(angles)[:, None, :]
    lower_half = values[..., :half_width]
    upper_half = values[..., half_width:]
    return jnp.concatenate([lower_half * cosine_table - upper_half * sine_table, upper_half * cosine_table + lower_half * sine_table], axis=-1)

def head_norm(projected, head_dim, scaling, positions):
    shaped = projected.reshape(projected.shape[0], -1, head_dim)
    return rotate(rms_norm(shaped, scaling), positions).astype(jnp.bfloat16)

def route_gates(normed, w_router, expert_ids):
    logits = jnp.dot(normed, w_router, preferred_element_type=jnp.float32)
    columns = jnp.arange(logits.shape[1], dtype=jnp.int32)
    picked = lax.optimization_barrier(jnp.sum(jnp.where(expert_ids[:, :, None] == columns[None, None, :], logits[:, None, :], 0.0), axis=2))
    return jax.nn.softmax(picked, axis=-1)

def slot_numbers(flat_ids, experts):
    columns = jnp.arange(experts, dtype=jnp.int32)
    onehot = (flat_ids[:, None] == columns[None, :]).astype(jnp.int32)
    return lax.optimization_barrier(jnp.sum((jnp.cumsum(onehot, axis=0) - onehot) * onehot, axis=1))

def reference(tokens, w_router, expert_ids, w_gate, w_up, w_down, moe_gain, attn_gain, w_query, w_key, w_value, w_out, q_gain, k_gain):
    token_total = tokens.shape[0]
    devices_all = N_CTX * N_KV
    normed = rms_norm(tokens, moe_gain).astype(jnp.bfloat16)
    gate_weights = route_gates(normed, w_router, expert_ids)
    flat_ids = expert_ids.reshape(devices_all, ROWS * TOP)
    slot_index = jax.vmap(lambda block_ids: slot_numbers(block_ids, EXPERTS))(flat_ids)
    sources = jnp.arange(devices_all, dtype=jnp.int32)[:, None]
    places = (flat_ids * (devices_all * CAP) + sources * CAP + slot_index).reshape(-1)
    entries = jnp.arange(token_total * TOP, dtype=jnp.int32)
    table = jnp.full((EXPERTS * devices_all * CAP,), token_total * TOP, jnp.int32).at[places].set(entries)
    table = table.reshape(EXPERTS, devices_all * CAP)
    padded_rows = jnp.concatenate([normed, jnp.zeros((1, D), jnp.bfloat16)], axis=0)
    flat_gates = jnp.concatenate([gate_weights.reshape(-1), jnp.zeros((1,), jnp.float32)])

    def one_expert(mixture, expert):
        entry_index = table[expert]
        token_index = entry_index // TOP
        token_rows = padded_rows[token_index]
        gate_part = jnp.dot(token_rows, w_gate[expert], preferred_element_type=jnp.float32)
        up_part = jnp.dot(token_rows, w_up[expert], preferred_element_type=jnp.float32)
        hidden = (jax.nn.silu(gate_part) * up_part).astype(jnp.bfloat16)
        out_rows = jnp.dot(hidden, w_down[expert], preferred_element_type=jnp.float32).astype(jnp.bfloat16)
        weighted = flat_gates[entry_index][:, None] * out_rows.astype(jnp.float32)
        return (mixture.at[token_index].add(weighted), None)
    mixture = lax.scan(one_expert, jnp.zeros((token_total + 1, D), jnp.float32), jnp.arange(EXPERTS, dtype=jnp.int32))[0]
    moe_out = (tokens.astype(jnp.float32) + mixture[:token_total]).astype(jnp.bfloat16)
    attn_in = rms_norm(moe_out, attn_gain).astype(jnp.bfloat16)
    positions = jnp.arange(token_total, dtype=jnp.int32)
    queries = head_norm(jnp.dot(attn_in, w_query, preferred_element_type=jnp.float32), HEAD_DIM, q_gain, positions)
    keys_all = head_norm(jnp.dot(attn_in, w_key, preferred_element_type=jnp.float32), HEAD_DIM, k_gain, positions)
    values_all = jnp.dot(attn_in, w_value, preferred_element_type=jnp.float32).astype(jnp.bfloat16).reshape(token_total, KV_HEADS, HEAD_DIM)
    span = (STOPS - 1) * SEQ_DEV
    keys_padded = jnp.concatenate([jnp.zeros((span, KV_HEADS, HEAD_DIM), jnp.bfloat16), keys_all], axis=0)
    values_padded = jnp.concatenate([jnp.zeros((span, KV_HEADS, HEAD_DIM), jnp.bfloat16), values_all], axis=0)
    group_size = HEADS // KV_HEADS
    query_blocks = queries.reshape(N_CTX, SEQ_DEV, KV_HEADS, group_size, HEAD_DIM)

    def attend(block):
        query_block = query_blocks[block].astype(jnp.float32)
        key_block = lax.dynamic_slice_in_dim(keys_padded, block * SEQ_DEV, STOPS * SEQ_DEV, 0).astype(jnp.float32)
        value_block = lax.dynamic_slice_in_dim(values_padded, block * SEQ_DEV, STOPS * SEQ_DEV, 0).astype(jnp.float32)
        scores = jnp.einsum('qngh,wnh->qngw', query_block, key_block) * HEAD_DIM ** (-0.5)
        query_pos = block * SEQ_DEV + jnp.arange(SEQ_DEV, dtype=jnp.int32)
        key_pos = block * SEQ_DEV - span + jnp.arange(STOPS * SEQ_DEV, dtype=jnp.int32)
        visible = (key_pos[None, :] >= 0) & (key_pos[None, :] <= query_pos[:, None])
        scores = jnp.where(visible[:, None, None, :], scores, MASKED)
        row_max = lax.optimization_barrier(jnp.max(scores, axis=3, keepdims=True))
        weights = jnp.exp(scores - row_max)
        denominator = lax.optimization_barrier(jnp.sum(weights, axis=3, keepdims=True))
        rounded = lax.optimization_barrier(weights.astype(jnp.bfloat16)).astype(jnp.float32)
        numerator = jnp.einsum('qngw,wnh->qngh', rounded, value_block)
        return (numerator / denominator).astype(jnp.bfloat16).reshape(SEQ_DEV, HEADS * HEAD_DIM)
    mixed_heads = lax.map(attend, jnp.arange(N_CTX, dtype=jnp.int32)).reshape(token_total, HEADS * HEAD_DIM)
    attended = jnp.dot(mixed_heads, w_out, preferred_element_type=jnp.float32).astype(jnp.bfloat16)
    return (moe_out, attended)
```

```python
import functools

import jax
import jax.numpy as jnp
from jax import lax
from jax.experimental import pallas as pl
from jax.experimental.pallas import tpu as pltpu
from jax.sharding import Mesh
from jax.sharding import PartitionSpec as P

STOPS = 8
EPSILON = 1e-06
THETA = 1000000.0
MASKED = -1e30
LOG2E = 1.4426950408889634


def rms_norm(values, scaling):
    values = values.astype(jnp.float32)
    inverse = lax.rsqrt(jnp.mean(values * values, axis=-1, keepdims=True) + EPSILON)
    return values * inverse * scaling


def rotate(values, positions):
    half_width = values.shape[-1] // 2
    frequency = THETA ** (-2.0 * jnp.arange(half_width, dtype=jnp.float32) / values.shape[-1])
    angles = positions.astype(jnp.float32)[:, None] * frequency[None, :]
    cosine_table = jnp.cos(angles)[:, None, :]
    sine_table = jnp.sin(angles)[:, None, :]
    lower_half = values[..., :half_width]
    upper_half = values[..., half_width:]
    return jnp.concatenate(
        [
            lower_half * cosine_table - upper_half * sine_table,
            upper_half * cosine_table + lower_half * sine_table,
        ],
        axis=-1,
    )


def head_norm(projected, head_dim, scaling, positions):
    shaped = projected.reshape(projected.shape[0], -1, head_dim)
    return rotate(rms_norm(shaped, scaling), positions).astype(jnp.bfloat16)


def moved(array, axis, by):
    size = lax.axis_size(axis)
    return lax.ppermute(array, axis, [(i, (i + by) % size) for i in range(size)])


def crossed(array, axis, bit):
    size = lax.axis_size(axis)
    return lax.ppermute(array, axis, [(i, i ^ bit) for i in range(size)])


def routing(ids, normed, w_router, first, plane_experts, capacity):
    rows = ids.shape[0]
    experts_all = w_router.shape[1]
    columns = jnp.arange(experts_all, dtype=jnp.int32)
    chosen = jnp.any(ids[None, :, :] == columns[:, None, None], axis=2)
    logits = lax.dot_general(
        w_router, normed, (((0,), (1,)), ((), ())), preferred_element_type=jnp.float32
    )
    largest = jnp.max(jnp.where(chosen, logits, MASKED), axis=0, keepdims=True)
    powers = jnp.where(chosen, jnp.exp(logits - largest), 0.0)
    gates = powers / jnp.sum(powers, axis=0, keepdims=True)
    gates = lax.dynamic_slice_in_dim(gates, first, plane_experts, 0)
    here = lax.dynamic_slice_in_dim(chosen.astype(jnp.bfloat16), first, plane_experts, 0)
    order = jnp.arange(rows, dtype=jnp.int32)
    before = (order[:, None] < order[None, :]).astype(jnp.bfloat16)
    rank = jnp.dot(here, before, preferred_element_type=jnp.float32).astype(jnp.int32)
    slots = jnp.arange(capacity, dtype=jnp.int32)
    select = (here[:, None, :] > 0) & (rank[:, None, :] == slots[None, :, None])
    weighted = jnp.where(select, gates[:, None, :], 0.0)
    upper = lax.reduce_precision(weighted, 8, 7)
    flat = (plane_experts * capacity, rows)
    return (
        select.astype(jnp.bfloat16).reshape(flat),
        upper.astype(jnp.bfloat16).reshape(flat),
        (weighted - upper).astype(jnp.bfloat16).reshape(flat),
    )


def expert_ffn(received, w_gate, w_up, w_down, capacity):
    pieces = []
    for x in range(w_gate.shape[0]):
        rows = received[:, x * capacity : (x + 1) * capacity].reshape(-1, received.shape[2])
        gate_part = jnp.dot(rows, w_gate[x], preferred_element_type=jnp.float32)
        up_part = jnp.dot(rows, w_up[x], preferred_element_type=jnp.float32)
        hidden = (jax.nn.silu(gate_part) * up_part).astype(jnp.bfloat16)
        out = jnp.dot(hidden, w_down[x], preferred_element_type=jnp.float32).astype(jnp.bfloat16)
        pieces.append(out.reshape(received.shape[0], capacity, -1))
    return pieces[0] if len(pieces) == 1 else jnp.concatenate(pieces, axis=1)


def attention_kernel(count, causal, carry, final, scale, *refs):
    refs = list(refs)
    flags_ref = refs.pop(0)
    q_ref = refs.pop(0)
    blocks = [refs.pop(0) for _ in range(count)]
    pos_q, pos_k = (refs.pop(0), refs.pop(0)) if causal else (None, None)
    if carry:
        acc_in, top_in = refs.pop(0), refs.pop(0)
    if final:
        out_ref = refs.pop(0)
        acc_ref, top_ref = refs.pop(0), refs.pop(0)
    else:
        acc_ref, top_ref = refs.pop(0), refs.pop(0)
    head_dim = q_ref.shape[1]
    rows = q_ref.shape[0]
    tile = min(rows, 256)
    factor = scale * LOG2E

    def update(block_ref, masked, fresh):
        keys = block_ref[0]
        values = jnp.concatenate([block_ref[1], jnp.ones_like(block_ref[1])], axis=1)
        for start in range(0, rows, tile):
            at = pl.ds(start, tile)
            scores = lax.dot_general(
                q_ref[at, :], keys, (((1,), (1,)), ((), ())), preferred_element_type=jnp.float32
            )
            if masked:
                scores = jnp.where(pos_k[...] <= pos_q[at, :], scores, MASKED)
            highest = jnp.max(scores, axis=1, keepdims=True)
            if fresh:
                top = highest
            else:
                top = jnp.maximum(top_ref[at, :1], highest)
            weights = jnp.exp2((scores - top) * factor).astype(jnp.bfloat16)
            added = jnp.dot(weights, values, preferred_element_type=jnp.float32)
            if not fresh:
                shrink = jnp.exp2((top_ref[at, :1] - top) * factor)
                added = acc_ref[at, :] * shrink + added
            acc_ref[at, :] = added
            top_ref[at, :] = jnp.broadcast_to(top, (tile, top_ref.shape[1]))

    if carry:
        acc_ref[...] = acc_in[...]
        top_ref[...] = top_in[...]
    for number, block_ref in enumerate(blocks):
        if causal and number == 0:
            update(block_ref, True, not carry)
        else:
            pl.when(flags_ref[number] > 0)(functools.partial(update, block_ref, False, False))
    if final:
        out_ref[...] = (acc_ref[:, :head_dim] / acc_ref[:, head_dim:]).astype(out_ref.dtype)


def attention(flags, queries, blocks, positions, carry, final, head_dim):
    rows, width = queries.shape
    group = width // head_dim
    keys = blocks[0].shape[1]
    head = lambda h: (0, h)
    whole3 = lambda h: (0, 0, 0)
    specs = [pl.BlockSpec(memory_space=pltpu.SMEM), pl.BlockSpec((rows, head_dim), head)]
    args = [flags, queries]
    for block in blocks:
        specs.append(pl.BlockSpec((2, keys, head_dim), whole3))
        args.append(block)
    causal = positions is not None
    if causal:
        specs += [pl.BlockSpec((rows, 1), lambda h: (0, 0)), pl.BlockSpec((1, keys), lambda h: (0, 0))]
        args += [positions[:, None], positions[None, :]]
    state_specs = [pl.BlockSpec((rows, 2 * head_dim), head), pl.BlockSpec((rows, head_dim), head)]
    state_shapes = [(rows, 2 * head_dim), (rows, head_dim)]
    if carry is not None:
        specs += state_specs
        args += list(carry)
    kernel = functools.partial(
        attention_kernel, len(blocks), causal, carry is not None, final, head_dim ** (-0.5)
    )
    if final:
        return pl.pallas_call(
            kernel,
            grid=(group,),
            in_specs=specs,
            out_specs=pl.BlockSpec((rows, head_dim), head),
            out_shape=jax.ShapeDtypeStruct((rows, width), jnp.bfloat16),
            scratch_shapes=[pltpu.VMEM(s, jnp.float32) for s in state_shapes],
            name="attention_last",
        )(*args)
    return pl.pallas_call(
        kernel,
        grid=(group,),
        in_specs=specs,
        out_specs=state_specs,
        out_shape=[jax.ShapeDtypeStruct((rows, s[1] * group), jnp.float32) for s in state_shapes],
        name="attention_first",
    )(*args)


def body(
    tokens,
    w_router,
    expert_ids,
    w_gate,
    w_up,
    w_down,
    moe_gain,
    attn_gain,
    w_query,
    w_key,
    w_value,
    w_out,
    q_gain,
    k_gain,
):
    row_count, model_width = tokens.shape
    top_count = expert_ids.shape[1]
    outer, inner, kv_size = lax.axis_size("outer"), lax.axis_size("inner"), lax.axis_size("kv")
    local_experts = w_gate.shape[0]
    experts_all = w_router.shape[1]
    plane = inner * kv_size
    plane_experts = plane * local_experts
    capacity = max(4, 5 * row_count * top_count // (4 * experts_all))
    outer_index = lax.axis_index("outer")
    inner_index = lax.axis_index("inner")
    kv_index = lax.axis_index("kv")
    first = outer_index * plane_experts

    exchange = functools.partial(
        lax.all_to_all, axis_name=("inner", "kv"), split_axis=0, concat_axis=0, tiled=True
    )
    shifts = [0] + sorted(range(1, outer), key=lambda s: (min(s, outer - s), s))
    ids = [moved(expert_ids, "outer", s) if s else expert_ids for s in shifts]
    rows = [moved(tokens, "outer", s) if s else tokens for s in shifts]
    own = None
    returned = []
    chunks = []
    for s, id_block, row_block in zip(shifts, ids, rows):
        normed = rms_norm(row_block, moe_gain).astype(jnp.bfloat16)
        select, upper, rest = routing(id_block, normed, w_router, first, plane_experts, capacity)
        outgoing = jnp.dot(select, normed, preferred_element_type=jnp.float32).astype(jnp.bfloat16)
        arrived = exchange(outgoing.reshape(plane, local_experts * capacity, model_width))
        computed = expert_ffn(arrived, w_gate, w_up, w_down, capacity)
        chunks.append((s, computed, upper, rest))
    for s, computed, upper, rest in chunks[1:] + chunks[:1]:
        back = exchange(computed).reshape(plane_experts * capacity, model_width)
        contract = (((0,), (0,)), ((), ()))
        partial = lax.dot_general(upper, back, contract, preferred_element_type=jnp.float32)
        partial += lax.dot_general(rest, back, contract, preferred_element_type=jnp.float32)
        if s:
            returned.append(moved(partial.astype(jnp.bfloat16), "outer", -s))
        else:
            own = partial
    total = tokens.astype(jnp.float32) + own
    for piece in returned:
        total += piece.astype(jnp.float32)
    moe_out = total.astype(jnp.bfloat16)

    bits = [1 << b for b in reversed(range((kv_size - 1).bit_length()))]
    gathered, pattern = moe_out, [0]
    for bit in bits:
        gathered = jnp.concatenate([gathered, crossed(gathered, "kv", bit)], axis=0)
        pattern = pattern + [p ^ bit for p in pattern]
    head_dim = q_gain.shape[0]
    seq_block = row_count * kv_size
    block_index = outer_index * inner + inner_index
    members = jnp.bitwise_xor(kv_index, jnp.array(pattern, dtype=jnp.int32))
    positions = (
        block_index * seq_block
        + members[:, None] * row_count
        + jnp.arange(row_count, dtype=jnp.int32)[None, :]
    ).reshape(-1)
    attn_in = rms_norm(gathered, attn_gain).astype(jnp.bfloat16)
    keys_new = head_norm(
        jnp.dot(attn_in, w_key, preferred_element_type=jnp.float32), head_dim, k_gain, positions
    ).reshape(seq_block, head_dim)
    values_new = jnp.dot(attn_in, w_value, preferred_element_type=jnp.float32).astype(jnp.bfloat16)
    own_block = jnp.stack([keys_new, values_new])
    queries = head_norm(
        jnp.dot(attn_in, w_query, preferred_element_type=jnp.float32), head_dim, q_gain, positions
    ).reshape(seq_block, -1)

    blocks, flags = [], []
    reach = min(outer - 1, (STOPS + inner - 2) // inner)
    columns = [own_block] + [
        lax.ppermute(own_block, "outer", [(i, i + m) for i in range(outer - m)])
        for m in range(1, reach + 1)
    ]
    for m, column in enumerate(columns):
        for step in range(inner):
            if m == 0 and step == 0:
                continue
            block = moved(column, "inner", step) if step else column
            source = (outer_index - m) * inner + (inner_index - step) % inner
            distance = block_index - source
            blocks.append(block)
            flags.append((source >= 0) & (distance > 0) & (distance < STOPS))
    flags = jnp.stack(flags).astype(jnp.int32) if flags else jnp.zeros((1,), jnp.int32)
    state = attention(flags, queries, [own_block], positions, None, not blocks, head_dim)
    mixed_heads = attention(flags, queries, blocks, None, state, True, head_dim) if blocks else state

    shares = jnp.dot(mixed_heads, w_out, preferred_element_type=jnp.float32)
    for bit in reversed(bits):
        half = shares.shape[0] // 2
        sent = crossed(shares[half:].astype(jnp.bfloat16), "kv", bit)
        shares = shares[:half] + sent.astype(jnp.float32)
    return (moe_out, shares.astype(jnp.bfloat16))


def solution(mesh):
    ctx_size, kv_size = mesh.shape["ctx"], mesh.shape["kv"]
    inner = 2 if ctx_size % 2 == 0 else 1
    fine = Mesh(mesh.devices.reshape(ctx_size // inner, inner, kv_size), ("outer", "inner", "kv"))
    every = ("outer", "inner", "kv")
    return jax.shard_map(
        body,
        mesh=fine,
        in_specs=(
            P(every, None),
            P(),
            P(every, None),
            P(every, None, None),
            P(every, None, None),
            P(every, None, None),
            P(),
            P(),
            P(None, "kv"),
            P(None, "kv"),
            P(None, "kv"),
            P("kv", None),
            P(),
            P(),
        ),
        out_specs=(P(every, None), P(every, None)),
        check_vma=False,
    )
```

```python
import functools

import jax
import jax.numpy as jnp
from jax import lax
from jax.experimental import pallas as pl
from jax.experimental.pallas import tpu as pltpu
from jax.sharding import Mesh
from jax.sharding import PartitionSpec as P

STOPS = 8
EPSILON = 1e-06
THETA = 1000000.0
MASKED = -1e30
LOG2E = 1.4426950408889634


def rms_norm(values, scaling):
    values = values.astype(jnp.float32)
    inverse = lax.rsqrt(jnp.mean(values * values, axis=-1, keepdims=True) + EPSILON)
    return values * inverse * scaling


def rotate(values, positions):
    half_width = values.shape[-1] // 2
    frequency = THETA ** (-2.0 * jnp.arange(half_width, dtype=jnp.float32) / values.shape[-1])
    angles = positions.astype(jnp.float32)[:, None] * frequency[None, :]
    cosine_table = jnp.cos(angles)[:, None, :]
    sine_table = jnp.sin(angles)[:, None, :]
    lower_half = values[..., :half_width]
    upper_half = values[..., half_width:]
    return jnp.concatenate(
        [
            lower_half * cosine_table - upper_half * sine_table,
            upper_half * cosine_table + lower_half * sine_table,
        ],
        axis=-1,
    )


def head_norm(projected, head_dim, scaling, positions):
    shaped = projected.reshape(projected.shape[0], -1, head_dim)
    return rotate(rms_norm(shaped, scaling), positions).astype(jnp.bfloat16)


def moved(array, axis, by):
    size = lax.axis_size(axis)
    return lax.ppermute(array, axis, [(i, (i + by) % size) for i in range(size)])


def crossed(array, axis, bit):
    size = lax.axis_size(axis)
    return lax.ppermute(array, axis, [(i, i ^ bit) for i in range(size)])


def routing(ids, normed, w_router, first, plane_experts, capacity):
    rows = ids.shape[0]
    experts_all = w_router.shape[1]
    columns = jnp.arange(experts_all, dtype=jnp.int32)
    chosen = jnp.any(ids[None, :, :] == columns[:, None, None], axis=2)
    logits = lax.dot_general(
        w_router, normed, (((0,), (1,)), ((), ())), preferred_element_type=jnp.float32
    )
    largest = jnp.max(jnp.where(chosen, logits, MASKED), axis=0, keepdims=True)
    powers = jnp.where(chosen, jnp.exp(logits - largest), 0.0)
    gates = powers / jnp.sum(powers, axis=0, keepdims=True)
    gates = lax.dynamic_slice_in_dim(gates, first, plane_experts, 0)
    here = lax.dynamic_slice_in_dim(chosen.astype(jnp.bfloat16), first, plane_experts, 0)
    order = jnp.arange(rows, dtype=jnp.int32)
    before = (order[:, None] < order[None, :]).astype(jnp.bfloat16)
    rank = jnp.dot(here, before, preferred_element_type=jnp.float32).astype(jnp.int32)
    slots = jnp.arange(capacity, dtype=jnp.int32)
    select = (here[:, None, :] > 0) & (rank[:, None, :] == slots[None, :, None])
    weighted = jnp.where(select, gates[:, None, :], 0.0)
    upper = lax.reduce_precision(weighted, 8, 7)
    flat = (plane_experts * capacity, rows)
    return (
        select.astype(jnp.bfloat16).reshape(flat),
        upper.astype(jnp.bfloat16).reshape(flat),
        (weighted - upper).astype(jnp.bfloat16).reshape(flat),
    )


def expert_ffn(received, w_gate, w_up, w_down, capacity):
    pieces = []
    for x in range(w_gate.shape[0]):
        rows = received[:, x * capacity : (x + 1) * capacity].reshape(-1, received.shape[2])
        gate_part = jnp.dot(rows, w_gate[x], preferred_element_type=jnp.float32)
        up_part = jnp.dot(rows, w_up[x], preferred_element_type=jnp.float32)
        hidden = (jax.nn.silu(gate_part) * up_part).astype(jnp.bfloat16)
        out = jnp.dot(hidden, w_down[x], preferred_element_type=jnp.float32).astype(jnp.bfloat16)
        pieces.append(out.reshape(received.shape[0], capacity, -1))
    return pieces[0] if len(pieces) == 1 else jnp.concatenate(pieces, axis=1)


def attention_kernel(count, group, scale, *refs):
    flags_ref, q_ref = refs[:2]
    blocks = refs[2 : 2 + count]
    pos_q, pos_k, out_ref, score_ref, top_ref, value_ref = refs[2 + count :]
    rows, keys = q_ref.shape[0], blocks[0].shape[1]
    head_dim = q_ref.shape[1] // group
    tile = score_ref.shape[1]
    lanes = top_ref.shape[2]
    tiles = rows // tile
    factor = scale * LOG2E
    for number, block_ref in enumerate(blocks):
        value_ref[number, :, :head_dim] = block_ref[1]
        value_ref[number, :, head_dim:] = jnp.ones((keys, head_dim), jnp.bfloat16)

    def score(query, at, number, top, slot):
        scores = lax.dot_general(
            query, blocks[number][0], (((1,), (1,)), ((), ())), preferred_element_type=jnp.float32
        )
        if number == 0:
            scores = jnp.where(pos_k[...] <= pos_q[at, :], scores, MASKED)
        score_ref[slot, :, pl.ds(number * keys, keys)] = scores
        highest = functools.reduce(
            jnp.maximum, [scores[:, i : i + lanes] for i in range(0, keys, lanes)]
        )
        if number:
            highest = jnp.where(flags_ref[number] > 0, highest, MASKED)
        return highest if top is None else jnp.maximum(top, highest)

    def weigh(number, top, total, slot):
        if number:
            top = jnp.where(flags_ref[number] > 0, top, -MASKED)
        top = jnp.concatenate([top] * (keys // lanes), axis=1)
        scores = score_ref[slot, :, pl.ds(number * keys, keys)]
        weights = jnp.exp2(scores * factor - top).astype(jnp.bfloat16)
        added = jnp.dot(weights, value_ref[number], preferred_element_type=jnp.float32)
        return added if total is None else total + added

    def settle(top, slot):
        top = jnp.max(top, axis=1, keepdims=True) * factor
        top_ref[slot] = jnp.broadcast_to(top, top_ref.shape[1:])

    def part(tile_number, head):
        at = pl.ds(tile_number * tile, tile)
        if not isinstance(head, int):
            head = pl.multiple_of(head * head_dim, head_dim)
        return at, pl.ds(head, head_dim)

    at, columns = part(0, 0)
    top = None
    for number in range(count):
        top = score(q_ref[at, columns], at, number, top, 0)
    settle(top, 0)

    def one_head(head, nothing):
        following = jnp.minimum(head + 1, group - 1)
        for number_of_tile in range(tiles):
            slot, other = number_of_tile % 2, (number_of_tile + 1) % 2
            last = number_of_tile + 1 == tiles
            at, columns = part(0 if last else number_of_tile + 1, following if last else head)
            query = q_ref[at, columns]
            settled = top_ref[slot]
            top, total = None, None
            for number in range(count):
                top = score(query, at, number, top, other)
                total = weigh(number, settled, total, slot)
            settle(top, other)
            at, columns = part(number_of_tile, head)
            out_ref[at, columns] = (total[:, :head_dim] / total[:, head_dim:]).astype(out_ref.dtype)
        return nothing

    lax.fori_loop(0, group, one_head, 0)


def attention(flags, queries, blocks, positions, head_dim):
    rows, width = queries.shape
    group = width // head_dim
    count, keys = len(blocks), blocks[0].shape[1]
    tile = rows // 2
    vmem = pl.BlockSpec(memory_space=pltpu.VMEM)
    return pl.pallas_call(
        functools.partial(attention_kernel, count, group, head_dim ** (-0.5)),
        in_specs=[pl.BlockSpec(memory_space=pltpu.SMEM)] + [vmem] * (count + 3),
        out_specs=vmem,
        out_shape=jax.ShapeDtypeStruct((rows, width), jnp.bfloat16),
        scratch_shapes=[
            pltpu.VMEM((2, tile, count * keys), jnp.float32),
            pltpu.VMEM((2, tile, 128), jnp.float32),
            pltpu.VMEM((count, keys, 2 * head_dim), jnp.bfloat16),
        ],
        name="attention",
    )(flags, queries, *blocks, positions[:, None], positions[None, :])


def body(
    tokens,
    w_router,
    expert_ids,
    w_gate,
    w_up,
    w_down,
    moe_gain,
    attn_gain,
    w_query,
    w_key,
    w_value,
    w_out,
    q_gain,
    k_gain,
):
    row_count, model_width = tokens.shape
    top_count = expert_ids.shape[1]
    outer, inner, kv_size = lax.axis_size("outer"), lax.axis_size("inner"), lax.axis_size("kv")
    local_experts = w_gate.shape[0]
    experts_all = w_router.shape[1]
    plane = inner * kv_size
    plane_experts = plane * local_experts
    capacity = max(4, 5 * row_count * top_count // (4 * experts_all))
    outer_index = lax.axis_index("outer")
    inner_index = lax.axis_index("inner")
    kv_index = lax.axis_index("kv")
    first = outer_index * plane_experts

    exchange = functools.partial(
        lax.all_to_all, axis_name=("inner", "kv"), split_axis=0, concat_axis=0, tiled=True
    )
    shifts = [0] + sorted(range(1, outer), key=lambda s: (min(s, outer - s), s))
    ids = [moved(expert_ids, "outer", s) if s else expert_ids for s in shifts]
    rows = [moved(tokens, "outer", s) if s else tokens for s in shifts]
    own = None
    returned = []
    chunks = []
    for s, id_block, row_block in zip(shifts, ids, rows):
        normed = rms_norm(row_block, moe_gain).astype(jnp.bfloat16)
        select, upper, rest = routing(id_block, normed, w_router, first, plane_experts, capacity)
        outgoing = jnp.dot(select, normed, preferred_element_type=jnp.float32).astype(jnp.bfloat16)
        arrived = exchange(outgoing.reshape(plane, local_experts * capacity, model_width))
        computed = expert_ffn(arrived, w_gate, w_up, w_down, capacity)
        chunks.append((s, computed, upper, rest))
    for s, computed, upper, rest in chunks[1:] + chunks[:1]:
        back = exchange(computed).reshape(plane_experts * capacity, model_width)
        contract = (((0,), (0,)), ((), ()))
        partial = lax.dot_general(upper, back, contract, preferred_element_type=jnp.float32)
        partial += lax.dot_general(rest, back, contract, preferred_element_type=jnp.float32)
        if s:
            returned.append(moved(partial.astype(jnp.bfloat16), "outer", -s))
        else:
            own = partial
    total = tokens.astype(jnp.float32) + own
    for piece in returned:
        total += piece.astype(jnp.float32)
    moe_out = total.astype(jnp.bfloat16)

    bits = [1 << b for b in reversed(range((kv_size - 1).bit_length()))]
    gathered, pattern = moe_out, [0]
    for bit in bits:
        gathered = jnp.concatenate([gathered, crossed(gathered, "kv", bit)], axis=0)
        pattern = pattern + [p ^ bit for p in pattern]
    head_dim = q_gain.shape[0]
    seq_block = row_count * kv_size
    block_index = outer_index * inner + inner_index
    members = jnp.bitwise_xor(kv_index, jnp.array(pattern, dtype=jnp.int32))
    positions = (
        block_index * seq_block
        + members[:, None] * row_count
        + jnp.arange(row_count, dtype=jnp.int32)[None, :]
    ).reshape(-1)
    attn_in = rms_norm(gathered, attn_gain).astype(jnp.bfloat16)
    keys_new = head_norm(
        jnp.dot(attn_in, w_key, preferred_element_type=jnp.float32), head_dim, k_gain, positions
    ).reshape(seq_block, head_dim)
    values_new = jnp.dot(attn_in, w_value, preferred_element_type=jnp.float32).astype(jnp.bfloat16)
    own_block = jnp.stack([keys_new, values_new])
    queries = head_norm(
        jnp.dot(attn_in, w_query, preferred_element_type=jnp.float32), head_dim, q_gain, positions
    ).reshape(seq_block, -1)

    blocks, flags = [], []
    reach = min(outer - 1, (STOPS + inner - 2) // inner)
    columns = [own_block] + [
        lax.ppermute(own_block, "outer", [(i, i + m) for i in range(outer - m)])
        for m in range(1, reach + 1)
    ]
    for m, column in enumerate(columns):
        for step in range(inner):
            block = moved(column, "inner", step) if step else column
            source = (outer_index - m) * inner + (inner_index - step) % inner
            distance = block_index - source
            blocks.append(block)
            flags.append((source >= 0) & (distance >= 0) & (distance < STOPS))
    flags = jnp.stack(flags).astype(jnp.int32)
    mixed_heads = attention(flags, queries, blocks, positions, head_dim)

    shares = jnp.dot(mixed_heads, w_out, preferred_element_type=jnp.float32)
    for bit in reversed(bits):
        half = shares.shape[0] // 2
        sent = crossed(shares[half:].astype(jnp.bfloat16), "kv", bit)
        shares = shares[:half] + sent.astype(jnp.float32)
    return (moe_out, shares.astype(jnp.bfloat16))


def solution(mesh):
    ctx_size, kv_size = mesh.shape["ctx"], mesh.shape["kv"]
    inner = 2 if ctx_size % 2 == 0 else 1
    fine = Mesh(mesh.devices.reshape(ctx_size // inner, inner, kv_size), ("outer", "inner", "kv"))
    every = ("outer", "inner", "kv")
    return jax.shard_map(
        body,
        mesh=fine,
        in_specs=(
            P(every, None),
            P(),
            P(every, None),
            P(every, None, None),
            P(every, None, None),
            P(every, None, None),
            P(),
            P(),
            P(None, "kv"),
            P(None, "kv"),
            P(None, "kv"),
            P("kv", None),
            P(),
            P(),
        ),
        out_specs=(P(every, None), P(every, None)),
        check_vma=False,
    )
```

```python
import functools

import jax
import jax.numpy as jnp
from jax import lax
from jax.experimental import pallas as pl
from jax.experimental.pallas import tpu as pltpu
from jax.sharding import Mesh
from jax.sharding import PartitionSpec as P

STOPS = 8
EPSILON = 1e-06
THETA = 1000000.0
MASKED = -1e30
LOG2E = 1.4426950408889634


def rms_norm(values, scaling):
    values = values.astype(jnp.float32)
    inverse = lax.rsqrt(jnp.mean(values * values, axis=-1, keepdims=True) + EPSILON)
    return values * inverse * scaling


def rotate(values, positions):
    half_width = values.shape[-1] // 2
    frequency = THETA ** (-2.0 * jnp.arange(half_width, dtype=jnp.float32) / values.shape[-1])
    angles = positions.astype(jnp.float32)[:, None] * frequency[None, :]
    cosine_table = jnp.cos(angles)[:, None, :]
    sine_table = jnp.sin(angles)[:, None, :]
    lower_half = values[..., :half_width]
    upper_half = values[..., half_width:]
    return jnp.concatenate(
        [
            lower_half * cosine_table - upper_half * sine_table,
            upper_half * cosine_table + lower_half * sine_table,
        ],
        axis=-1,
    )


def head_norm(projected, head_dim, scaling, positions):
    shaped = projected.reshape(projected.shape[0], -1, head_dim)
    return rotate(rms_norm(shaped, scaling), positions).astype(jnp.bfloat16)


def moved(array, axis, by):
    size = lax.axis_size(axis)
    return lax.ppermute(array, axis, [(i, (i + by) % size) for i in range(size)])


def crossed(array, axis, bit):
    size = lax.axis_size(axis)
    return lax.ppermute(array, axis, [(i, i ^ bit) for i in range(size)])


def select_kernel(count, capacity, *refs):
    scalar_ref, ids_ref, router_ref, gain_ref = refs[:4]
    token_refs = refs[4 : 4 + count]
    sends = refs[4 + count : -3]
    upper_ref, rest_ref, normed_ref = refs[-3:]
    rows = token_refs[0].shape[0]
    experts = router_ref.shape[0]
    wanted = scalar_ref.shape[0] - count
    columns = lax.broadcasted_iota(jnp.int32, (experts, rows), 0)
    slots = lax.broadcasted_iota(jnp.int32, (capacity, rows), 0).astype(jnp.float32)
    before = (
        lax.broadcasted_iota(jnp.int32, (rows, rows), 0)
        < lax.broadcasted_iota(jnp.int32, (rows, rows), 1)
    ).astype(jnp.bfloat16)
    picks = [[None] * count for _ in range(wanted)]
    for number, token_ref in enumerate(token_refs):
        values = token_ref[...].astype(jnp.float32)
        inverse = lax.rsqrt(jnp.mean(values * values, axis=1, keepdims=True) + EPSILON)
        normed = (values * inverse * gain_ref[...]).astype(jnp.bfloat16)
        normed_ref[pl.ds(number * rows, rows), :] = normed
        logits = lax.dot_general(
            router_ref[...], normed, (((1,), (1,)), ((), ())), preferred_element_type=jnp.float32
        )
        ids = ids_ref[scalar_ref[number]]
        chosen = columns == ids[:1]
        for choice in range(1, ids.shape[0]):
            chosen = chosen | (columns == ids[choice : choice + 1])
        largest = jnp.max(jnp.where(chosen, logits, MASKED), axis=0, keepdims=True)
        powers = jnp.where(chosen, jnp.exp(logits - largest), 0.0)
        gates = powers / jnp.sum(powers, axis=0, keepdims=True)
        chosen = chosen.astype(jnp.float32)
        for want in range(wanted):
            mine = columns == scalar_ref[count + want]
            here = jnp.sum(jnp.where(mine, chosen, 0.0), axis=0, keepdims=True)
            gate = jnp.sum(jnp.where(mine, gates, 0.0), axis=0, keepdims=True)
            rank = jnp.dot(
                jnp.broadcast_to(here, (16, rows)).astype(jnp.bfloat16),
                before,
                preferred_element_type=jnp.float32,
            )[:1]
            select = jnp.where((slots == rank) & (here > 0), 1.0, 0.0)
            parts = [jnp.zeros_like(select)] * count
            parts[number] = select
            weights = [jnp.zeros_like(select)] * count
            weights[number] = select * gate
            picks[want][number] = (
                jnp.concatenate(parts, axis=1),
                jnp.concatenate(weights, axis=1),
            )
    flat = [pick for row in picks for pick in row]
    select = jnp.concatenate([pick[0] for pick in flat], axis=0).astype(jnp.bfloat16)
    weights = jnp.concatenate([pick[1] for pick in flat], axis=0)
    upper = weights.astype(jnp.bfloat16)
    upper_ref[...] = upper
    rest_ref[...] = (weights - upper.astype(jnp.float32)).astype(jnp.bfloat16)
    share = select.shape[0] // len(sends)
    for number, send_ref in enumerate(sends):
        send_ref[...] = jnp.dot(
            select[number * share : (number + 1) * share],
            normed_ref[...],
            preferred_element_type=jnp.float32,
        ).astype(jnp.bfloat16)


def select_rows(scalars, ids, router, gain, blocks, members, capacity):
    rows, width = blocks[0].shape
    count = len(blocks)
    slots = (scalars.shape[0] - count) * count * capacity
    vmem = pl.BlockSpec(memory_space=pltpu.VMEM)
    result = pl.pallas_call(
        functools.partial(select_kernel, count, capacity),
        in_specs=[pl.BlockSpec(memory_space=pltpu.SMEM)] + [vmem] * (3 + count),
        out_specs=[vmem] * (members + 2),
        out_shape=[jax.ShapeDtypeStruct((slots // members, width), jnp.bfloat16)] * members
        + [jax.ShapeDtypeStruct((slots, count * rows), jnp.bfloat16)] * 2,
        scratch_shapes=[pltpu.VMEM((count * rows, width), jnp.bfloat16)],
        name="select_rows",
    )(scalars, ids, router, gain, *blocks)
    return result[:members], result[members:]


def expert_kernel(members, *refs):
    arrived = refs[:members]
    gate_ref, up_ref, down_ref = refs[members : members + 3]
    outs = refs[members + 3 : -1]
    rows_ref = refs[-1]
    share = arrived[0].shape[0]
    experts = gate_ref.shape[0]
    part = share // experts
    for x in range(experts):
        for number, piece in enumerate(arrived):
            rows_ref[pl.ds(number * part, part), :] = piece[pl.ds(x * part, part), :]
        rows = rows_ref[...]
        gate = jnp.dot(rows, gate_ref[x], preferred_element_type=jnp.float32)
        up = jnp.dot(rows, up_ref[x], preferred_element_type=jnp.float32)
        hidden = (jax.nn.silu(gate) * up).astype(jnp.bfloat16)
        out = jnp.dot(hidden, down_ref[x], preferred_element_type=jnp.float32).astype(jnp.bfloat16)
        for number, piece in enumerate(outs):
            piece[pl.ds(x * part, part), :] = out[number * part : (number + 1) * part]


def expert_rows(arrived, w_gate, w_up, w_down):
    members = len(arrived)
    share, width = arrived[0].shape
    vmem = pl.BlockSpec(memory_space=pltpu.VMEM)
    return pl.pallas_call(
        functools.partial(expert_kernel, members),
        in_specs=[vmem] * (members + 3),
        out_specs=[vmem] * members,
        out_shape=[jax.ShapeDtypeStruct((share, width), jnp.bfloat16)] * members,
        scratch_shapes=[pltpu.VMEM((members * share // w_gate.shape[0], width), jnp.bfloat16)],
        name="expert_rows",
    )(*arrived, w_gate, w_up, w_down)


def mix_kernel(members, upper_ref, rest_ref, *refs):
    arrived, outs, rows_ref = refs[:members], refs[members:-1], refs[-1]
    share = arrived[0].shape[0]
    for number, piece in enumerate(arrived):
        rows_ref[pl.ds(number * share, share), :] = piece[...]
    contract = (((0,), (0,)), ((), ()))
    rows = rows_ref[...]
    total = lax.dot_general(upper_ref[...], rows, contract, preferred_element_type=jnp.float32)
    total += lax.dot_general(rest_ref[...], rows, contract, preferred_element_type=jnp.float32)
    length = outs[0].shape[0]
    for number, out_ref in enumerate(outs):
        out_ref[...] = total[number * length : (number + 1) * length].astype(out_ref.dtype)


def mix_rows(weights, arrived, count):
    share, width = arrived[0].shape
    length = weights[0].shape[1] // count
    vmem = pl.BlockSpec(memory_space=pltpu.VMEM)
    return pl.pallas_call(
        functools.partial(mix_kernel, len(arrived)),
        in_specs=[vmem] * (2 + len(arrived)),
        out_specs=[vmem] * count,
        out_shape=[
            jax.ShapeDtypeStruct((length, width), jnp.bfloat16 if b else jnp.float32)
            for b in range(count)
        ],
        scratch_shapes=[pltpu.VMEM((len(arrived) * share, width), jnp.bfloat16)],
        name="mix_rows",
    )(*weights, *arrived)


def attention_kernel(count, group, scale, *refs):
    flags_ref, q_ref = refs[:2]
    blocks = refs[2 : 2 + count]
    pos_q, pos_k, out_ref, score_ref, top_ref, value_ref = refs[2 + count :]
    rows, keys = q_ref.shape[0], blocks[0].shape[1]
    head_dim = q_ref.shape[1] // group
    tile = score_ref.shape[1]
    lanes = top_ref.shape[2]
    tiles = rows // tile
    factor = scale * LOG2E
    for number, block_ref in enumerate(blocks):
        value_ref[number, :, :head_dim] = block_ref[1]
        value_ref[number, :, head_dim:] = jnp.ones((keys, head_dim), jnp.bfloat16)

    def score(query, at, number, top, slot):
        scores = lax.dot_general(
            query, blocks[number][0], (((1,), (1,)), ((), ())), preferred_element_type=jnp.float32
        )
        if number == 0:
            scores = jnp.where(pos_k[...] <= pos_q[at, :], scores, MASKED)
        score_ref[slot, :, pl.ds(number * keys, keys)] = scores
        highest = functools.reduce(
            jnp.maximum, [scores[:, i : i + lanes] for i in range(0, keys, lanes)]
        )
        if number:
            highest = jnp.where(flags_ref[number] > 0, highest, MASKED)
        return highest if top is None else jnp.maximum(top, highest)

    def weigh(number, top, total, slot):
        if number:
            top = jnp.where(flags_ref[number] > 0, top, -MASKED)
        top = jnp.concatenate([top] * (keys // lanes), axis=1)
        scores = score_ref[slot, :, pl.ds(number * keys, keys)]
        weights = jnp.exp2(scores * factor - top).astype(jnp.bfloat16)
        added = jnp.dot(weights, value_ref[number], preferred_element_type=jnp.float32)
        return added if total is None else total + added

    def settle(top, slot):
        top = jnp.max(top, axis=1, keepdims=True) * factor
        top_ref[slot] = jnp.broadcast_to(top, top_ref.shape[1:])

    def part(tile_number, head):
        at = pl.ds(tile_number * tile, tile)
        if not isinstance(head, int):
            head = pl.multiple_of(head * head_dim, head_dim)
        return at, pl.ds(head, head_dim)

    at, columns = part(0, 0)
    top = None
    for number in range(count):
        top = score(q_ref[at, columns], at, number, top, 0)
    settle(top, 0)

    def one_head(head, nothing):
        following = jnp.minimum(head + 1, group - 1)
        for number_of_tile in range(tiles):
            slot, other = number_of_tile % 2, (number_of_tile + 1) % 2
            last = number_of_tile + 1 == tiles
            at, columns = part(0 if last else number_of_tile + 1, following if last else head)
            query = q_ref[at, columns]
            settled = top_ref[slot]
            top, total = None, None
            for number in range(count):
                top = score(query, at, number, top, other)
                total = weigh(number, settled, total, slot)
            settle(top, other)
            at, columns = part(number_of_tile, head)
            out_ref[at, columns] = (total[:, :head_dim] / total[:, head_dim:]).astype(out_ref.dtype)
        return nothing

    lax.fori_loop(0, group, one_head, 0)


def attention(flags, queries, blocks, positions, head_dim):
    rows, width = queries.shape
    group = width // head_dim
    count, keys = len(blocks), blocks[0].shape[1]
    tile = rows // 2
    vmem = pl.BlockSpec(memory_space=pltpu.VMEM)
    return pl.pallas_call(
        functools.partial(attention_kernel, count, group, head_dim ** (-0.5)),
        in_specs=[pl.BlockSpec(memory_space=pltpu.SMEM)] + [vmem] * (count + 3),
        out_specs=vmem,
        out_shape=jax.ShapeDtypeStruct((rows, width), jnp.bfloat16),
        scratch_shapes=[
            pltpu.VMEM((2, tile, count * keys), jnp.float32),
            pltpu.VMEM((2, tile, 128), jnp.float32),
            pltpu.VMEM((count, keys, 2 * head_dim), jnp.bfloat16),
        ],
        name="attention",
    )(flags, queries, *blocks, positions[:, None], positions[None, :])


def body(
    tokens,
    w_router,
    expert_ids,
    w_gate,
    w_up,
    w_down,
    moe_gain,
    attn_gain,
    w_query,
    w_key,
    w_value,
    w_out,
    q_gain,
    k_gain,
):
    row_count, model_width = tokens.shape
    top_count = expert_ids.shape[1]
    outer, inner, kv_size = lax.axis_size("outer"), lax.axis_size("inner"), lax.axis_size("kv")
    local_experts = w_gate.shape[0]
    experts_all = w_router.shape[1]
    capacity = max(4, 5 * row_count * top_count // (4 * experts_all))
    capacity = (capacity + 7) // 8 * 8
    outer_index = lax.axis_index("outer")
    inner_index = lax.axis_index("inner")
    kv_index = lax.axis_index("kv")
    block_index = outer_index * inner + inner_index

    ids = jnp.broadcast_to(expert_ids.T[None], (outer * inner, top_count, row_count))
    ids = lax.all_to_all(ids, ("outer", "inner"), split_axis=0, concat_axis=0, tiled=True)
    members = jnp.bitwise_xor(kv_index, jnp.arange(kv_size, dtype=jnp.int32))
    wanted = (
        (block_index * kv_size + members)[:, None] * local_experts
        + jnp.arange(local_experts, dtype=jnp.int32)[None, :]
    ).reshape(-1)
    router = w_router.T
    gain = moe_gain[None, :]
    shifts = [0] + sorted(range(1, outer), key=lambda s: (min(s, outer - s), s))
    columns = [moved(tokens, "outer", s) if s else tokens for s in shifts]
    state = []
    for s, column in zip(shifts, columns):
        blocks = [moved(column, "inner", t) if t else column for t in range(inner)]
        sources = jnp.stack(
            [
                (outer_index - s) % outer * inner + (inner_index - t) % inner
                for t in range(inner)
            ]
        )
        scalars = jnp.concatenate([sources.astype(jnp.int32), wanted.astype(jnp.int32)])
        sends, weights = select_rows(scalars, ids, router, gain, blocks, kv_size, capacity)
        arrived = [crossed(rows, "kv", j) if j else rows for j, rows in enumerate(sends)]
        state.append((s, expert_rows(arrived, w_gate, w_up, w_down), weights))
    total = tokens.astype(jnp.float32)
    for s, computed, weights in state[1:] + state[:1]:
        arrived = [crossed(rows, "kv", j) if j else rows for j, rows in enumerate(computed)]
        sums = mix_rows(weights, arrived, inner)
        here = sums[0]
        for t in range(1, inner):
            here += moved(sums[t], "inner", -t).astype(jnp.float32)
        if s:
            here = moved(here.astype(jnp.bfloat16), "outer", -s).astype(jnp.float32)
        total += here
    moe_out = total.astype(jnp.bfloat16)

    bits = [1 << b for b in reversed(range((kv_size - 1).bit_length()))]
    gathered, pattern = moe_out, [0]
    for bit in bits:
        gathered = jnp.concatenate([gathered, crossed(gathered, "kv", bit)], axis=0)
        pattern = pattern + [p ^ bit for p in pattern]
    head_dim = q_gain.shape[0]
    seq_block = row_count * kv_size
    members = jnp.bitwise_xor(kv_index, jnp.array(pattern, dtype=jnp.int32))
    positions = (
        block_index * seq_block
        + members[:, None] * row_count
        + jnp.arange(row_count, dtype=jnp.int32)[None, :]
    ).reshape(-1)
    attn_in = rms_norm(gathered, attn_gain).astype(jnp.bfloat16)
    keys_new = head_norm(
        jnp.dot(attn_in, w_key, preferred_element_type=jnp.float32), head_dim, k_gain, positions
    ).reshape(seq_block, head_dim)
    values_new = jnp.dot(attn_in, w_value, preferred_element_type=jnp.float32).astype(jnp.bfloat16)
    own_block = jnp.stack([keys_new, values_new])
    queries = head_norm(
        jnp.dot(attn_in, w_query, preferred_element_type=jnp.float32), head_dim, q_gain, positions
    ).reshape(seq_block, -1)

    blocks, flags = [], []
    reach = min(outer - 1, (STOPS + inner - 2) // inner)
    columns = [own_block] + [
        lax.ppermute(own_block, "outer", [(i, i + m) for i in range(outer - m)])
        for m in range(1, reach + 1)
    ]
    for m, column in enumerate(columns):
        for step in range(inner):
            block = moved(column, "inner", step) if step else column
            source = (outer_index - m) * inner + (inner_index - step) % inner
            distance = block_index - source
            blocks.append(block)
            flags.append((source >= 0) & (distance >= 0) & (distance < STOPS))
    flags = jnp.stack(flags).astype(jnp.int32)
    mixed_heads = attention(flags, queries, blocks, positions, head_dim)

    shares = jnp.dot(mixed_heads, w_out, preferred_element_type=jnp.float32)
    for bit in reversed(bits):
        half = shares.shape[0] // 2
        sent = crossed(shares[half:].astype(jnp.bfloat16), "kv", bit)
        shares = shares[:half] + sent.astype(jnp.float32)
    return (moe_out, shares.astype(jnp.bfloat16))


def solution(mesh):
    ctx_size, kv_size = mesh.shape["ctx"], mesh.shape["kv"]
    inner = 2 if ctx_size % 2 == 0 else 1
    fine = Mesh(mesh.devices.reshape(ctx_size // inner, inner, kv_size), ("outer", "inner", "kv"))
    every = ("outer", "inner", "kv")
    return jax.shard_map(
        body,
        mesh=fine,
        in_specs=(
            P(every, None),
            P(),
            P(every, None),
            P(every, None, None),
            P(every, None, None),
            P(every, None, None),
            P(),
            P(),
            P(None, "kv"),
            P(None, "kv"),
            P(None, "kv"),
            P("kv", None),
            P(),
            P(),
        ),
        out_specs=(P(every, None), P(every, None)),
        check_vma=False,
    )
```
